32 devices in a mesh: dp: 8 (over z, x), mp: 4 (over y, core).
Axes of the slice: x: 2, y: 2, z: 4, core: 2. Of those that a mesh axis runs over, the one named last changes fastest.
Arguments:
- tokens: bfloat16 [2048, 8192], P('dp', 'mp'), may hold values from -6 to 6
- cotangent: bfloat16 [2048, 8192], P('dp', 'mp'), may hold values from -6 to 6
- w_in: bfloat16 [64, 4, 256, 256], P('mp'), may hold values from -0.1875 to 0.1875
- w_out: bfloat16 [64, 4, 256, 256], P('mp'), may hold values from -0.125 to 0.125
- in_blocks: int32 [64, 4], P('mp'), may hold values from 0 to 31, as said below
- out_blocks: int32 [64, 4], P('mp'), may hold values from 0 to 31, as said below
Outputs:
- output: bfloat16 [2048, 8192], P('dp', 'mp')
- grad_tokens: bfloat16 [2048, 8192], P('dp', 'mp')
- grad_in: float32 [64, 4, 256, 256], P('mp', None, 'dp')
- grad_out: float32 [64, 4, 256, 256], P('mp', None, 'dp')
The draws below stay inside these ranges and needn't reach their ends.
Inputs may be any that keep to these rules, and one draw needn't show every extreme that they name: `in_blocks`: flat butterfly pattern: row j holds p(j mod 32 XOR m) for m = 0, 1, 2, 4, with p a permutation of the 32 input blocks; the 4 entries of a row differ and every block is named by exactly 8 rows. `out_blocks`: the same flat butterfly form with its own permutation q of the 32 output blocks.
All inputs are finite; a program needn't handle non-finite values.
Results may differ from the reference program's by a relative error of at most 0.018.
Values may be sent and summed in bfloat16 or wider, within the bound.
A program may use at most 128 MiB of HBM per device.

```python
import jax
import jax.numpy as jnp
from jax import lax

D = 8192
BS = 256
K = 4
RB = 32
HB = 64
TOKENS = 2048
N_MP = 4


def butterfly_lists(key, salt):
    order = jax.random.permutation(jax.random.fold_in(key, salt), RB).astype(jnp.int32)
    base = jnp.arange(HB, dtype=jnp.int32) % RB
    masks = jnp.array([0, 1, 2, 4], dtype=jnp.int32)
    return order[jnp.bitwise_xor(base[:, None], masks[None, :])].astype(jnp.int32)


def draw_in_blocks(key, part):
    return butterfly_lists(key, 11)


def draw_out_blocks(key, part):
    return butterfly_lists(key, 23)


def block_scale(rng, shape, split, smallest, largest):
    level, own = 1.0, jax.random.fold_in(rng, 6)
    for position, shards_of in split:
        heights = jnp.exp(jax.random.uniform(jax.random.fold_in(own, position), (shards_of,), jnp.float32, smallest / len(split), largest / len(split)))
        level = level * jnp.repeat(heights, shape[position] // shards_of).reshape([-1 if axis == position else 1 for axis in range(len(shape))])
    return level


def gaussian(key, shape, width, limit, pieces=(), held_as=jnp.bfloat16):
    result = width * jax.random.normal(key, shape, jnp.float32)
    if pieces:
        result = result * block_scale(key, shape, pieces, -0.22, 0.18)
    return jnp.clip(result, -limit, limit).astype(held_as)


def setup_inputs(seed: int = 0) -> dict:
    streams_of = jax.random.split(jax.random.key(seed), 7)
    tokens = gaussian(streams_of[0], (TOKENS, D), 1.0, 6.0, ((0, 8), (1, 4)))
    cotangent = gaussian(streams_of[1], (TOKENS, D), 1.0, 6.0, ((0, 8), (1, 4)))
    w_in = gaussian(streams_of[2], (HB, K, BS, BS), (K * BS) ** -0.5, 0.1875, ((0, 4),))
    w_out = gaussian(streams_of[3], (HB, K, BS, BS), (HB * K * BS // RB) ** -0.5, 0.125, ((0, 4),))
    in_blocks = draw_in_blocks(jax.random.fold_in(streams_of[6], 71), 0)
    out_blocks = draw_out_blocks(jax.random.fold_in(streams_of[6], 71), 0)
    return dict(tokens=tokens, cotangent=cotangent, w_in=w_in, w_out=w_out, in_blocks=in_blocks, out_blocks=out_blocks)


def reference(tokens, cotangent, w_in, w_out, in_blocks, out_blocks):
    total = tokens.shape[0]
    group_size = HB // N_MP
    token_blocks = tokens.reshape(total, RB, BS)
    cot_blocks = cotangent.reshape(total, RB, BS)
    w_in_g = w_in.reshape(N_MP, group_size, K, BS, BS)
    w_out_g = w_out.reshape(N_MP, group_size, K, BS, BS)
    in_g = in_blocks.reshape(N_MP, group_size, K).astype(jnp.int32)
    out_g = out_blocks.reshape(N_MP, group_size, K).astype(jnp.int32)

    def group(carry, items):
        out_acc, back_acc = carry
        weight_in, weight_out, idx_in, idx_out = items
        selected = token_blocks[:, idx_in].astype(jnp.float32)
        pre = jnp.einsum('tjkb,jkbc->tjc', selected, weight_in.astype(jnp.float32))
        act = jax.nn.gelu(pre).astype(jnp.bfloat16)
        terms = jnp.einsum('tjb,jkbc->tjkc', act.astype(jnp.float32), weight_out.astype(jnp.float32))
        part = jnp.zeros((total, RB, BS), jnp.float32).at[:, idx_out.reshape(-1)].add(terms.reshape(total, group_size * K, BS))
        part = lax.optimization_barrier(part.reshape(total, D).astype(jnp.bfloat16)).astype(jnp.float32)
        picked = cot_blocks[:, idx_out].astype(jnp.float32)
        d_act = jnp.einsum('tjkc,jkbc->tjb', picked, weight_out.astype(jnp.float32))
        _, pullback = jax.vjp(jax.nn.gelu, pre)
        d_pre = pullback(d_act)[0].astype(jnp.bfloat16)
        grad_o = jnp.einsum('tjb,tjkc->jkbc', act.astype(jnp.float32), picked)
        grad_i = jnp.einsum('tjkb,tjc->jkbc', selected, d_pre.astype(jnp.float32))
        back = jnp.einsum('tjc,jkbc->tjkb', d_pre.astype(jnp.float32), weight_in.astype(jnp.float32))
        back_part = jnp.zeros((total, RB, BS), jnp.float32).at[:, idx_in.reshape(-1)].add(back.reshape(total, group_size * K, BS))
        back_part = lax.optimization_barrier(back_part.reshape(total, D).astype(jnp.bfloat16)).astype(jnp.float32)
        return ((out_acc + part, back_acc + back_part), (grad_i, grad_o))
    start = (jnp.zeros((total, D), jnp.float32), jnp.zeros((total, D), jnp.float32))
    (out_acc, back_acc), (grads_i, grads_o) = lax.scan(group, start, (w_in_g, w_out_g, in_g, out_g))
    scale = 1.0 / jnp.sqrt(jnp.float32(TOKENS))
    grad_in = grads_i.reshape(HB, K, BS, BS) * scale
    grad_out = grads_o.reshape(HB, K, BS, BS) * scale
    return (out_acc.astype(jnp.bfloat16), back_acc.astype(jnp.bfloat16), grad_in, grad_out)
```

```python
import functools
import math

import jax
import jax.numpy as jnp
from jax import lax
from jax.experimental import pallas as pl
from jax.experimental.pallas import tpu as pltpu
from jax.sharding import PartitionSpec as P

MB = 2
MASKS = (0, 1, 2, 4)
MESH = pl.DeviceIdType.MESH
C0 = math.sqrt(2.0 / math.pi)
C1 = 0.044715


def place_blocks(values, targets, row_blocks):
    step_tok = values.shape[0]
    side = values.shape[-1]
    flat = values.reshape(step_tok, -1, side)
    placed = (
        jnp.zeros((step_tok, row_blocks, side), jnp.float32).at[:, targets.reshape(-1)].add(flat)
    )
    return placed.reshape(step_tok, row_blocks * side)


def shards_plain(tokens, cotangent, w_in, w_out, in_blocks, out_blocks):
    hb_dev, kk, side, _ = w_in.shape
    total_tok = tokens.shape[0]
    width = tokens.shape[1] * lax.axis_size("mp")
    row_blocks = width // side
    passes = MB
    step_tok = total_tok // passes
    grad_in = jnp.zeros(w_in.shape, jnp.float32)
    grad_out = jnp.zeros(w_out.shape, jnp.float32)
    out_share = None
    outputs = []
    backs = []
    for index in range(passes):
        x_part = tokens[index * step_tok : (index + 1) * step_tok]
        dy_part = cotangent[index * step_tok : (index + 1) * step_tok]
        x_full = lax.all_gather(x_part, "mp", axis=1, tiled=True)
        selected = x_full.reshape(step_tok, row_blocks, side)[:, in_blocks]
        pre = jnp.einsum("tjkb,jkbc->tjc", selected, w_in, preferred_element_type=jnp.float32)
        act = jax.nn.gelu(pre).astype(jnp.bfloat16)
        terms = jnp.einsum("tjb,jkbc->tjkc", act, w_out, preferred_element_type=jnp.float32)
        partial_out = place_blocks(terms, out_blocks, row_blocks)
        outputs.append(
            lax.psum_scatter(
                partial_out.astype(jnp.bfloat16), "mp", scatter_dimension=1, tiled=True
            )
        )
        dy_full = lax.all_gather(dy_part, "mp", axis=1, tiled=True)
        picked = dy_full.reshape(step_tok, row_blocks, side)[:, out_blocks]
        d_act = jnp.einsum("tjkc,jkbc->tjb", picked, w_out, preferred_element_type=jnp.float32)
        _, pullback = jax.vjp(jax.nn.gelu, pre)
        d_pre = pullback(d_act)[0].astype(jnp.bfloat16)
        grad_out = grad_out + jnp.einsum(
            "tjb,tjkc->jkbc", act, picked, preferred_element_type=jnp.float32
        )
        grad_in = grad_in + jnp.einsum(
            "tjkb,tjc->jkbc", selected, d_pre, preferred_element_type=jnp.float32
        )
        back = jnp.einsum("tjc,jkbc->tjkb", d_pre, w_in, preferred_element_type=jnp.float32)
        partial_back = place_blocks(back, in_blocks, row_blocks)
        backs.append(
            lax.psum_scatter(
                partial_back.astype(jnp.bfloat16), "mp", scatter_dimension=1, tiled=True
            )
        )
    scale = 1.0 / math.sqrt(total_tok * lax.axis_size("dp"))
    in_share, out_share = (
        lax.psum_scatter(
            grad_in.astype(jnp.bfloat16), "dp", scatter_dimension=2, tiled=True
        ).astype(jnp.float32),
        lax.psum_scatter(
            grad_out.astype(jnp.bfloat16), "dp", scatter_dimension=2, tiled=True
        ).astype(jnp.float32),
    )
    output = jnp.concatenate(outputs, axis=0)
    grad_tokens = jnp.concatenate(backs, axis=0)
    return (output, grad_tokens, in_share * scale, out_share * scale)


def flip(u, m):
    if m == 0:
        return u
    return u + m * (1 - 2 * ((u // m) % 2))


def dot(a, b, dims):
    return lax.dot_general(a, b, (dims, ((), ())), preferred_element_type=jnp.float32)


def fused_kernel(
    dims,
    in_idx, out_idx, in_inv, out_inv, x_hbm, dy_hbm, win_hbm, wout_hbm,
    part, red,
    full, grads, arrived, act, dpre, wbuf, acc, csend, crecv,
    own_sem, y_send, y_recv, c_send, c_recv, f_send, f_recv,
    w_sem, g_send, g_recv, z_send, z_recv, zl_sem,
    o_send, o_recv, p_send, p_recv, pl_sem,
):
    ndp, nmp, hb, side, own, tok, rows = dims
    nz = ndp // 2
    dp = lax.axis_index("dp")
    mp = lax.axis_index("mp")
    z, mx = dp // 2, dp % 2
    y, core = mp // 2, mp % 2
    other_core = (dp, y * 2 + 1 - core)
    other_y = (dp, (1 - y) * 2 + core)
    other_x = (z * 2 + 1 - mx, mp)
    g_core = other_core[1]
    g_y = other_y[1]
    g_far = (1 - y) * 2 + 1 - core
    srcs = (x_hbm, dy_hbm)

    def z_peer(dz):
        return (z + dz) % nz

    barrier = pltpu.get_barrier_semaphore()
    peers = [other_core, other_y, other_x] + [(z_peer(dz) * 2 + mx, mp) for dz in range(1, nz)]
    for peer in peers:
        pl.semaphore_signal(barrier, inc=1, device_id=peer, device_id_type=MESH)
    pl.semaphore_wait(barrier, len(peers))

    def remote(src, dst, ssem, rsem, peer):
        return pltpu.make_async_remote_copy(
            src_ref=src, dst_ref=dst, send_sem=ssem, recv_sem=rsem,
            device_id=peer, device_id_type=MESH,
        )

    def piece(a, i):
        return srcs[a].at[:, pl.ds(pl.multiple_of(i * side, side), side)]

    def to_y(a, i, slot):
        return remote(piece(a, i), full.at[a, slot * own + i], y_send.at[a, i], y_recv.at[a, i], other_y)

    def to_core(a, i, slot):
        return remote(piece(a, i), full.at[a, slot * own + i], c_send.at[a, i], c_recv.at[a, i], other_core)

    def forward(a, i, slot):
        return remote(
            full.at[a, g_y * own + i], full.at[a, slot * own + i],
            f_send.at[a, i], f_recv.at[a, i], other_core,
        )

    def keep(a, i):
        return pltpu.make_async_copy(piece(a, i), full.at[a, mp * own + i], own_sem.at[a, i])

    def w_copies(j, slot):
        return (
            pltpu.make_async_copy(win_hbm.at[j], wbuf.at[slot, 0], w_sem.at[slot, 0, 0]),
            pltpu.make_async_copy(wout_hbm.at[j], wbuf.at[slot, 1], w_sem.at[slot, 1, 0]),
        )

    def loop(n, body):
        lax.fori_loop(0, n, lambda i, c: (body(i), c)[1], 0)

    for a in range(2):
        def start(i, a=a):
            to_y(a, i, mp).start()
            to_core(a, i, mp).start()
            keep(a, i).start()
        loop(own, start)
    for cp in w_copies(0, 0):
        cp.start()
    for a in range(2):
        def relay(i, a=a):
            to_y(a, i, g_y).wait_recv()
            forward(a, i, g_y).start()
        loop(own, relay)
    for a in range(2):
        def settle(i, a=a):
            keep(a, i).wait()
            to_core(a, i, g_core).wait_recv()
            forward(a, i, g_far).wait_recv()
        loop(own, settle)

    def hidden(j):
        slot = j % 2
        for cp in w_copies(j, slot):
            cp.wait()

        @pl.when(j + 1 < hb)
        def _():
            for cp in w_copies(j + 1, 1 - slot):
                cp.start()

        pre = jnp.zeros((tok, side), jnp.float32)
        d_act = jnp.zeros((tok, side), jnp.float32)
        for k in range(len(MASKS)):
            pre += dot(full[0, in_idx[j, k]], wbuf[slot, 0, k], ((1,), (0,)))
            d_act += dot(full[1, out_idx[j, k]], wbuf[slot, 1, k], ((1,), (1,)))
        th = jnp.tanh(C0 * (pre + C1 * (pre * pre * pre)))
        half = 0.5 * (1.0 + th)
        slope = half + 0.5 * pre * (1.0 - th * th) * (C0 * (1.0 + 3.0 * C1 * pre * pre))
        act[j] = (pre * half).astype(jnp.bfloat16)
        dpre[j] = (d_act * slope).astype(jnp.bfloat16)

    loop(hb, hidden)

    def to_x(j):
        return remote(grads.at[j, 1 - mx], arrived.at[j], g_send.at[j], g_recv.at[j], other_x)

    def weight_grads(j):
        for k in range(len(MASKS)):
            gi = dot(full[0, in_idx[j, k]], dpre[j], ((0,), (0,)))
            go = dot(act[j], full[1, out_idx[j, k]], ((0,), (0,)))
            for a, value in ((0, gi), (1, go)):
                value = value.astype(jnp.bfloat16).reshape(nz, 2, rows, side)
                for xx in range(2):
                    grads[j, xx, a, k] = value[:, xx]
        to_x(j).start()

    loop(hb, weight_grads)

    def v_copies(u, slot):
        res = []
        for k, m in enumerate(MASKS):
            v = flip(u, m)
            res.append(pltpu.make_async_copy(win_hbm.at[v, k], wbuf.at[slot, 0, k], w_sem.at[slot, 0, k]))
            res.append(pltpu.make_async_copy(wout_hbm.at[v, k], wbuf.at[slot, 1, k], w_sem.at[slot, 1, k]))
        return res

    for cp in v_copies(0, 0):
        cp.start()

    def place(u):
        slot = u % 2
        for cp in v_copies(u, slot):
            cp.wait()

        @pl.when(u + 1 < hb)
        def _():
            for cp in v_copies(u + 1, 1 - slot):
                cp.start()

        out = jnp.zeros((tok, side), jnp.float32)
        back = jnp.zeros((tok, side), jnp.float32)
        for k, m in enumerate(MASKS):
            v = flip(u, m)
            out += dot(act[v], wbuf[slot, 1, k], ((1,), (0,)))
            back += dot(dpre[v], wbuf[slot, 0, k], ((1,), (1,)))
        acc[0, u] = out.astype(jnp.bfloat16)
        acc[1, u] = back.astype(jnp.bfloat16)

    loop(hb, place)
    inv = (out_inv, in_inv)
    for a in range(2):
        acc[a, hb] = jnp.zeros((tok, side), jnp.bfloat16)

    def swap(a):
        return remote(csend.at[a], crecv.at[a], o_send.at[a], o_recv.at[a], other_core)

    for a in range(2):
        for yy in range(2):
            def fill(i, a=a, yy=yy):
                csend[a, yy, i] = acc[a, inv[a][(2 * yy + 1 - core) * own + i]]
            loop(own, fill)
        swap(a).start()

    def to_part(a):
        return remote(crecv.at[a, 1 - y], part.at[a, 1], p_send.at[a], p_recv.at[a], other_y)

    def keep_part(a):
        return pltpu.make_async_copy(crecv.at[a, y], part.at[a, 0], pl_sem.at[a])

    for a in range(2):
        swap(a).wait_recv()
        for yy in range(2):
            def join(i, a=a, yy=yy):
                crecv[a, yy, i] = crecv[a, yy, i] + acc[a, inv[a][(2 * yy + core) * own + i]]
            loop(own, join)
        to_part(a).start()
        keep_part(a).start()

    def to_z(j, dz, slot):
        return remote(
            grads.at[j, mx, :, :, z_peer(dz)], red.at[slot, :, j],
            z_send.at[dz - 1, j], z_recv.at[dz - 1, j], (z_peer(dz) * 2 + mx, mp),
        )

    def keep_z(j):
        return pltpu.make_async_copy(grads.at[j, mx, :, :, z], red.at[z, :, j], zl_sem.at[j])

    def pair_sum(j):
        to_x(j).wait_recv()
        for a in range(2):
            for k in range(len(MASKS)):
                grads[j, mx, a, k] = (
                    grads[j, mx, a, k].astype(jnp.float32) + arrived[j, a, k].astype(jnp.float32)
                ).astype(jnp.bfloat16)
        for dz in range(1, nz):
            to_z(j, dz, z).start()
        keep_z(j).start()

    loop(hb, pair_sum)

    for a in range(2):
        def drain(i, a=a):
            to_y(a, i, mp).wait_send()
            to_core(a, i, mp).wait_send()
            forward(a, i, g_y).wait_send()
        loop(own, drain)
        swap(a).wait_send()
        to_part(a).wait_send()
        to_part(a).wait_recv()
        keep_part(a).wait()

    def finish(j):
        to_x(j).wait_send()
        keep_z(j).wait()
        for dz in range(1, nz):
            to_z(j, dz, z).wait_send()
            to_z(j, dz, (z - dz + nz) % nz).wait_recv()

    loop(hb, finish)


def shards_fused(ndp, nmp, tokens, cotangent, w_in, w_out, in_blocks, out_blocks):
    hb, kk, side, _ = w_in.shape
    tok, feats = tokens.shape
    own = feats // side
    blocks = own * nmp
    nz = ndp // 2
    rows = side // ndp

    def inverse(table):
        hit = table[:, 0][None, :] == jnp.arange(blocks, dtype=jnp.int32)[:, None]
        where = jnp.sum(jnp.where(hit, jnp.arange(hb, dtype=jnp.int32)[None, :], 0), axis=1)
        return jnp.where(jnp.any(hit, axis=1), where, hb).astype(jnp.int32)

    bf = jnp.bfloat16
    any_spec = pl.BlockSpec(memory_space=pl.ANY)
    smem = pl.BlockSpec(memory_space=pltpu.SMEM)
    dma = pltpu.SemaphoreType.DMA
    part, red = pl.pallas_call(
        functools.partial(fused_kernel, (ndp, nmp, hb, side, own, tok, rows)),
        out_shape=(
            jax.ShapeDtypeStruct((2, 2, own, tok, side), bf),
            jax.ShapeDtypeStruct((nz, 2, hb, kk, rows, side), bf),
        ),
        in_specs=[smem] * 4 + [any_spec] * 4,
        out_specs=(any_spec, any_spec),
        scratch_shapes=[
            pltpu.VMEM((2, blocks, tok, side), bf),
            pltpu.VMEM((hb, 2, 2, kk, nz, rows, side), bf),
            pltpu.VMEM((hb, 2, kk, nz, rows, side), bf),
            pltpu.VMEM((hb, tok, side), bf),
            pltpu.VMEM((hb, tok, side), bf),
            pltpu.VMEM((2, 2, kk, side, side), bf),
            pltpu.VMEM((2, hb + 1, tok, side), bf),
            pltpu.VMEM((2, 2, own, tok, side), bf),
            pltpu.VMEM((2, 2, own, tok, side), bf),
        ]
        + [dma((2, own))] * 7
        + [dma((2, 2, kk)), dma((hb,)), dma((hb,)), dma((nz - 1, hb)), dma((nz - 1, hb)), dma((hb,))]
        + [dma((2,))] * 5,
        compiler_params=pltpu.CompilerParams(
            collective_id=0, has_side_effects=True, vmem_limit_bytes=66_000_000
        ),
    )(
        in_blocks, out_blocks, inverse(in_blocks), inverse(out_blocks),
        tokens, cotangent, w_in, w_out,
    )
    scale = 1.0 / math.sqrt(tok * ndp)
    both = part[:, 0].astype(jnp.float32) + part[:, 1].astype(jnp.float32)
    both = both.astype(bf).transpose(0, 2, 1, 3).reshape(2, tok, feats)
    total = red.astype(jnp.float32).sum(axis=0) * scale
    return both[0], both[1], total[0], total[1]


def solution(mesh):
    ndp, nmp = mesh.shape["dp"], mesh.shape["mp"]

    def shards(tokens, cotangent, w_in, w_out, in_blocks, out_blocks):
        hb, kk, side, _ = w_in.shape
        blocks = tokens.shape[1] * nmp // side
        fits = (
            nmp == 4
            and ndp % 2 == 0
            and kk == len(MASKS)
            and 2 * hb == blocks
            and hb % 8 == 0
            and side % (16 * ndp) == 0
        )
        args = (tokens, cotangent, w_in, w_out, in_blocks, out_blocks)
        if fits:
            return shards_fused(ndp, nmp, *args)
        return shards_plain(*args)

    placed = (
        P("dp", "mp"),
        P("dp", "mp"),
        P("mp", None, None, None),
        P("mp", None, None, None),
        P("mp", None),
        P("mp", None),
    )
    return jax.shard_map(
        shards,
        mesh=mesh,
        in_specs=placed,
        out_specs=(
            P("dp", "mp"),
            P("dp", "mp"),
            P("mp", None, "dp", None),
            P("mp", None, "dp", None),
        ),
        check_vma=False,
    )
```

```python
import functools
import math

import jax
import jax.numpy as jnp
from jax import lax
from jax.experimental import pallas as pl
from jax.experimental.pallas import tpu as pltpu
from jax.sharding import PartitionSpec as P

MB = 2
MASKS = (0, 1, 2, 4)
MESH = pl.DeviceIdType.MESH
C0 = math.sqrt(2.0 / math.pi)
C1 = 0.044715
SKEW = 2


def place_blocks(values, targets, row_blocks):
    step_tok = values.shape[0]
    side = values.shape[-1]
    flat = values.reshape(step_tok, -1, side)
    placed = (
        jnp.zeros((step_tok, row_blocks, side), jnp.float32).at[:, targets.reshape(-1)].add(flat)
    )
    return placed.reshape(step_tok, row_blocks * side)


def shards_plain(tokens, cotangent, w_in, w_out, in_blocks, out_blocks):
    hb_dev, kk, side, _ = w_in.shape
    total_tok = tokens.shape[0]
    width = tokens.shape[1] * lax.axis_size("mp")
    row_blocks = width // side
    passes = MB
    step_tok = total_tok // passes
    grad_in = jnp.zeros(w_in.shape, jnp.float32)
    grad_out = jnp.zeros(w_out.shape, jnp.float32)
    out_share = None
    outputs = []
    backs = []
    for index in range(passes):
        x_part = tokens[index * step_tok : (index + 1) * step_tok]
        dy_part = cotangent[index * step_tok : (index + 1) * step_tok]
        x_full = lax.all_gather(x_part, "mp", axis=1, tiled=True)
        selected = x_full.reshape(step_tok, row_blocks, side)[:, in_blocks]
        pre = jnp.einsum("tjkb,jkbc->tjc", selected, w_in, preferred_element_type=jnp.float32)
        act = jax.nn.gelu(pre).astype(jnp.bfloat16)
        terms = jnp.einsum("tjb,jkbc->tjkc", act, w_out, preferred_element_type=jnp.float32)
        partial_out = place_blocks(terms, out_blocks, row_blocks)
        outputs.append(
            lax.psum_scatter(
                partial_out.astype(jnp.bfloat16), "mp", scatter_dimension=1, tiled=True
            )
        )
        dy_full = lax.all_gather(dy_part, "mp", axis=1, tiled=True)
        picked = dy_full.reshape(step_tok, row_blocks, side)[:, out_blocks]
        d_act = jnp.einsum("tjkc,jkbc->tjb", picked, w_out, preferred_element_type=jnp.float32)
        _, pullback = jax.vjp(jax.nn.gelu, pre)
        d_pre = pullback(d_act)[0].astype(jnp.bfloat16)
        grad_out = grad_out + jnp.einsum(
            "tjb,tjkc->jkbc", act, picked, preferred_element_type=jnp.float32
        )
        grad_in = grad_in + jnp.einsum(
            "tjkb,tjc->jkbc", selected, d_pre, preferred_element_type=jnp.float32
        )
        back = jnp.einsum("tjc,jkbc->tjkb", d_pre, w_in, preferred_element_type=jnp.float32)
        partial_back = place_blocks(back, in_blocks, row_blocks)
        backs.append(
            lax.psum_scatter(
                partial_back.astype(jnp.bfloat16), "mp", scatter_dimension=1, tiled=True
            )
        )
    scale = 1.0 / math.sqrt(total_tok * lax.axis_size("dp"))
    in_share, out_share = (
        lax.psum_scatter(
            grad_in.astype(jnp.bfloat16), "dp", scatter_dimension=2, tiled=True
        ).astype(jnp.float32),
        lax.psum_scatter(
            grad_out.astype(jnp.bfloat16), "dp", scatter_dimension=2, tiled=True
        ).astype(jnp.float32),
    )
    output = jnp.concatenate(outputs, axis=0)
    grad_tokens = jnp.concatenate(backs, axis=0)
    return (output, grad_tokens, in_share * scale, out_share * scale)


def flip(u, m):
    if m == 0:
        return u
    return u + m * (1 - 2 * ((u // m) % 2))


def dot(a, b, dims):
    return lax.dot_general(a, b, (dims, ((), ())), preferred_element_type=jnp.float32)


def fused_kernel(
    dims,
    in_idx, out_idx, in_inv, out_inv, x_hbm, dy_hbm, win_hbm, wout_hbm,
    part_out, part_back, red,
    full, near, mine, theirs, arrived, act, dpre, act2, dpre2, wbuf, acc, csend, crecv, zbuf,
    own_sem, y_send, y_recv, c_send, c_recv, f_send, f_recv,
    x_send, x_recv, y2_send, y2_recv, c2_send, c2_recv, f2_send, f2_recv,
    p_send, p_recv, pl_sem,
    w_sem, g_send, g_recv, up_send, up_recv, dn_send, dn_recv, zl_sem,
    o_send, o_recv,
):
    ndp, nmp, hb, side, own, tok, rows, n1 = dims
    nz = ndp // 2
    dp = lax.axis_index("dp")
    mp = lax.axis_index("mp")
    z, mx = dp // 2, dp % 2
    y, core = mp // 2, mp % 2
    other_core = (dp, y * 2 + 1 - core)
    other_y = (dp, (1 - y) * 2 + core)
    other_x = (z * 2 + 1 - mx, mp)
    above = ((dp + 2) % ndp, mp)
    below = ((dp + ndp - 2) % ndp, mp)
    has_above = z < nz - 1
    has_below = z > 0
    g_core = other_core[1]
    g_y = other_y[1]
    g_far = (1 - y) * 2 + 1 - core
    srcs = (x_hbm, dy_hbm)
    parts = (part_out, part_back)
    nk = len(MASKS)

    barrier = pltpu.get_barrier_semaphore()
    peers = [other_core, other_y, other_x] + [((dp + 2 * dz) % ndp, mp) for dz in range(1, nz)]
    for peer in peers:
        pl.semaphore_signal(barrier, inc=1, device_id=peer, device_id_type=MESH)
    pl.semaphore_wait(barrier, len(peers))

    def remote(src, dst, ssem, rsem, peer):
        return pltpu.make_async_remote_copy(
            src_ref=src, dst_ref=dst, send_sem=ssem, recv_sem=rsem,
            device_id=peer, device_id_type=MESH,
        )

    def lanes(i):
        return pl.ds(pl.multiple_of(i * side, side), side)

    def piece(a, i):
        return srcs[a].at[:, lanes(i)]

    def to_y(a, i, slot):
        return remote(piece(a, i), full.at[a, slot * own + i], y_send.at[a, i], y_recv.at[a, i], other_y)

    def to_core(a, i, slot):
        return remote(piece(a, i), full.at[a, slot * own + i], c_send.at[a, i], c_recv.at[a, i], other_core)

    def forward(a, i, slot):
        return remote(
            full.at[a, g_y * own + i], full.at[a, slot * own + i],
            f_send.at[a, i], f_recv.at[a, i], other_core,
        )

    def to_near(a, i):
        return remote(piece(a, i), near.at[a, mp * own + i], x_send.at[a, i], x_recv.at[a, i], other_x)

    def near_y(a, i, slot):
        return remote(
            near.at[a, mp * own + i], near.at[a, slot * own + i],
            y2_send.at[a, i], y2_recv.at[a, i], other_y,
        )

    def near_core(a, i, slot):
        return remote(
            near.at[a, mp * own + i], near.at[a, slot * own + i],
            c2_send.at[a, i], c2_recv.at[a, i], other_core,
        )

    def near_forward(a, i, slot):
        return remote(
            near.at[a, g_y * own + i], near.at[a, slot * own + i],
            f2_send.at[a, i], f2_recv.at[a, i], other_core,
        )

    def keep(a, i):
        return pltpu.make_async_copy(piece(a, i), full.at[a, mp * own + i], own_sem.at[a, i])

    def w_copies(j, slot):
        return (
            pltpu.make_async_copy(win_hbm.at[j], wbuf.at[slot, 0], w_sem.at[slot, 0, 0]),
            pltpu.make_async_copy(wout_hbm.at[j], wbuf.at[slot, 1], w_sem.at[slot, 1, 0]),
        )

    def loop(n, body, first=0):
        lax.fori_loop(first, n, lambda i, c: (body(i), c)[1], 0)

    for a in range(2):
        def start(i, a=a):
            to_y(a, i, mp).start()
            to_near(a, i).start()
            to_core(a, i, mp).start()
            keep(a, i).start()
        loop(own, start)
    for cp in w_copies(0, 0):
        cp.start()
    for a in range(2):
        def relay(i, a=a):
            to_y(a, i, g_y).wait_recv()
            forward(a, i, g_y).start()
            to_near(a, i).wait_recv()
            near_y(a, i, mp).start()
            near_core(a, i, mp).start()
        loop(own, relay)
    for a in range(2):
        def settle(i, a=a):
            keep(a, i).wait()
            to_core(a, i, g_core).wait_recv()
            forward(a, i, g_far).wait_recv()
        loop(own, settle)

    def hidden_of(source, act_ref, dpre_ref):
        def hidden(j):
            slot = j % 2
            for cp in w_copies(j, slot):
                cp.wait()

            @pl.when(j + 1 < hb)
            def _():
                for cp in w_copies(j + 1, 1 - slot):
                    cp.start()

            pre = jnp.zeros((tok, side), jnp.float32)
            d_act = jnp.zeros((tok, side), jnp.float32)
            for k in range(nk):
                pre += dot(source[0, in_idx[j, k]], wbuf[slot, 0, k], ((1,), (0,)))
                d_act += dot(source[1, out_idx[j, k]], wbuf[slot, 1, k], ((1,), (1,)))
            th = jnp.tanh(C0 * (pre + C1 * (pre * pre * pre)))
            half = 0.5 * (1.0 + th)
            slope = half + 0.5 * pre * (1.0 - th * th) * (C0 * (1.0 + 3.0 * C1 * pre * pre))
            act_ref[j] = (pre * half).astype(jnp.bfloat16)
            dpre_ref[j] = (d_act * slope).astype(jnp.bfloat16)

        loop(hb, hidden)

    hidden_of(full, act, dpre)

    def to_x(j):
        return remote(theirs.at[j], arrived.at[j], g_send.at[j], g_recv.at[j], other_x)

    def split(value):
        value = value.astype(jnp.bfloat16).reshape(nz, 2, rows, side)
        low, high = value[:, 0], value[:, 1]
        return jnp.where(mx == 0, low, high), jnp.where(mx == 0, high, low)

    def weight_grads(j):
        for k in range(nk):
            gi = dot(full[0, in_idx[j, k]], dpre[j], ((0,), (0,)))
            go = dot(act[j], full[1, out_idx[j, k]], ((0,), (0,)))
            for a, value in ((0, gi), (1, go)):
                mine_half, their_half = split(value)
                mine[j, a, k] = mine_half
                theirs[j, a, k] = their_half
        to_x(j).start()

    loop(n1, weight_grads)

    def v_copies(u, slot):
        res = []
        for k, m in enumerate(MASKS):
            v = flip(u, m)
            res.append(pltpu.make_async_copy(win_hbm.at[v, k], wbuf.at[slot, 0, k], w_sem.at[slot, 0, k]))
            res.append(pltpu.make_async_copy(wout_hbm.at[v, k], wbuf.at[slot, 1, k], w_sem.at[slot, 1, k]))
        return res

    for cp in v_copies(0, 0):
        cp.start()

    def place(u):
        slot = u % 2
        for cp in v_copies(u, slot):
            cp.wait()

        @pl.when(u + 1 < hb)
        def _():
            for cp in v_copies(u + 1, 1 - slot):
                cp.start()

        out = jnp.zeros((tok, side), jnp.float32)
        back = jnp.zeros((tok, side), jnp.float32)
        for k, m in enumerate(MASKS):
            v = flip(u, m)
            out += dot(act[v], wbuf[slot, 1, k], ((1,), (0,)))
            back += dot(dpre[v], wbuf[slot, 0, k], ((1,), (1,)))
        acc[0, u] = out.astype(jnp.bfloat16)
        acc[1, u] = back.astype(jnp.bfloat16)

    loop(hb, place)
    for cp in w_copies(0, 0):
        cp.start()
    inv = (out_inv, in_inv)
    for a in range(2):
        acc[a, hb] = jnp.zeros((tok, side), jnp.bfloat16)

    def swap(a):
        return remote(csend.at[a], crecv.at[a], o_send.at[a], o_recv.at[a], other_core)

    for a in range(2):
        for yy in range(2):
            def fill(i, a=a, yy=yy):
                csend[a, yy, i] = acc[a, inv[a][(2 * yy + 1 - core) * own + i]]
            loop(own, fill)
        swap(a).start()

    def to_part(a, i):
        return remote(
            crecv.at[a, 1 - y, i], parts[a].at[1, :, lanes(i)], p_send.at[a, i], p_recv.at[a, i], other_y
        )

    def keep_part(a, i):
        return pltpu.make_async_copy(crecv.at[a, y, i], parts[a].at[0, :, lanes(i)], pl_sem.at[a, i])

    for a in range(2):
        swap(a).wait_recv()
        for yy in range(2):
            def join(i, a=a, yy=yy):
                crecv[a, yy, i] = crecv[a, yy, i] + acc[a, inv[a][(2 * yy + core) * own + i]]
            loop(own, join)

        def emit(i, a=a):
            to_part(a, i).start()
            keep_part(a, i).start()
        loop(own, emit)

    def up(j, u, last):
        dst = red.at[1, :, j] if last else zbuf.at[u - 1, j]
        return remote(mine.at[j, :, :, u], dst, up_send.at[u - 1, j], up_recv.at[u - 1, j], above)

    def down(j, u, last):
        dst = red.at[2, :, j] if last else zbuf.at[u, j]
        return remote(mine.at[j, :, :, u], dst, dn_send.at[u, j], dn_recv.at[u, j], below)

    def keep_z(j):
        return pltpu.make_async_copy(mine.at[j, :, :, z], red.at[0, :, j], zl_sem.at[j])

    def add_in(j, u, slot):
        for a in range(2):
            mine[j, a, :, u] = (
                mine[j, a, :, u].astype(jnp.float32) + zbuf[slot, j, a].astype(jnp.float32)
            ).astype(jnp.bfloat16)

    def hops(t):
        ju = t - SKEW * z
        jd = t - SKEW * (nz - 1 - z)
        up_ok = jnp.logical_and(ju >= 0, ju < hb)
        dn_ok = jnp.logical_and(jd >= 0, jd < hb)
        for u in range(nz - 1, 0, -1):
            @pl.when(jnp.logical_and(up_ok, z < u))
            def _(u=u):
                @pl.when(has_below)
                def _():
                    up(ju, u, False).wait_recv()
                    add_in(ju, u, u - 1)

                @pl.when(z == u - 1)
                def _():
                    up(ju, u, True).start()

                @pl.when(z < u - 1)
                def _():
                    up(ju, u, False).start()
        for u in range(nz - 1):
            @pl.when(jnp.logical_and(dn_ok, z > u))
            def _(u=u):
                @pl.when(has_above)
                def _():
                    down(jd, u, False).wait_recv()
                    add_in(jd, u, u)

                @pl.when(z == u + 1)
                def _():
                    down(jd, u, True).start()

                @pl.when(z > u + 1)
                def _():
                    down(jd, u, False).start()

    def first_steps(t):
        to_x(t).wait_recv()
        for a in range(2):
            for k in range(nk):
                mine[t, a, k] = (
                    mine[t, a, k].astype(jnp.float32) + arrived[t, a, k].astype(jnp.float32)
                ).astype(jnp.bfloat16)
        keep_z(t).start()
        hops(t)

    loop(n1, first_steps)

    for a in range(2):
        def relay2(i, a=a):
            near_y(a, i, g_y).wait_recv()
            near_forward(a, i, g_y).start()
        loop(own, relay2)
    for a in range(2):
        def settle2(i, a=a):
            near_core(a, i, g_core).wait_recv()
            near_forward(a, i, g_far).wait_recv()
        loop(own, settle2)

    hidden_of(near, act2, dpre2)

    def later_steps(t):
        for k in range(nk):
            gi = dot(full[0, in_idx[t, k]], dpre[t], ((0,), (0,)))
            gi += dot(near[0, in_idx[t, k]], dpre2[t], ((0,), (0,)))
            go = dot(act[t], full[1, out_idx[t, k]], ((0,), (0,)))
            go += dot(act2[t], near[1, out_idx[t, k]], ((0,), (0,)))
            mine[t, 0, k] = split(gi)[0]
            mine[t, 1, k] = split(go)[0]
        keep_z(t).start()
        hops(t)

    loop(hb, later_steps, n1)
    loop(hb + SKEW * (nz - 2), hops, hb)

    for a in range(2):
        def drain(i, a=a):
            to_y(a, i, mp).wait_send()
            to_core(a, i, mp).wait_send()
            forward(a, i, g_y).wait_send()
            to_near(a, i).wait_send()
            near_y(a, i, mp).wait_send()
            near_core(a, i, mp).wait_send()
            near_forward(a, i, g_y).wait_send()
            to_part(a, i).wait_send()
            to_part(a, i).wait_recv()
            keep_part(a, i).wait()
        loop(own, drain)
        swap(a).wait_send()

    def sent(j):
        to_x(j).wait_send()

    loop(n1, sent)

    def finish(j):
        keep_z(j).wait()
        for u in range(1, nz):
            @pl.when(z < u)
            def _(u=u):
                up(j, u, True).wait_send()

            @pl.when(z == u)
            def _(u=u):
                up(j, u, True).wait_recv()
        for u in range(nz - 1):
            @pl.when(z > u)
            def _(u=u):
                down(j, u, True).wait_send()

            @pl.when(z == u)
            def _(u=u):
                down(j, u, True).wait_recv()

    loop(hb, finish)


def shards_fused(ndp, nmp, tokens, cotangent, w_in, w_out, in_blocks, out_blocks):
    hb, kk, side, _ = w_in.shape
    tok, feats = tokens.shape
    own = feats // side
    blocks = own * nmp
    nz = ndp // 2
    rows = side // ndp
    n1 = hb // 4

    def inverse(table):
        hit = table[:, 0][None, :] == jnp.arange(blocks, dtype=jnp.int32)[:, None]
        where = jnp.sum(jnp.where(hit, jnp.arange(hb, dtype=jnp.int32)[None, :], 0), axis=1)
        return jnp.where(jnp.any(hit, axis=1), where, hb).astype(jnp.int32)

    bf = jnp.bfloat16
    any_spec = pl.BlockSpec(memory_space=pl.ANY)
    smem = pl.BlockSpec(memory_space=pltpu.SMEM)
    dma = pltpu.SemaphoreType.DMA
    part_out, part_back, red = pl.pallas_call(
        functools.partial(fused_kernel, (ndp, nmp, hb, side, own, tok, rows, n1)),
        out_shape=(
            jax.ShapeDtypeStruct((2, tok, feats), bf),
            jax.ShapeDtypeStruct((2, tok, feats), bf),
            jax.ShapeDtypeStruct((3, 2, hb, kk, rows, side), bf),
        ),
        in_specs=[smem] * 4 + [any_spec] * 4,
        out_specs=(any_spec,) * 3,
        scratch_shapes=[
            pltpu.VMEM((2, blocks, tok, side), bf),
            pltpu.VMEM((2, blocks, tok, side), bf),
            pltpu.VMEM((hb, 2, kk, nz, rows, side), bf),
            pltpu.VMEM((n1, 2, kk, nz, rows, side), bf),
            pltpu.VMEM((n1, 2, kk, nz, rows, side), bf),
            pltpu.VMEM((hb, tok, side), bf),
            pltpu.VMEM((hb, tok, side), bf),
            pltpu.VMEM((hb, tok, side), bf),
            pltpu.VMEM((hb, tok, side), bf),
            pltpu.VMEM((2, 2, kk, side, side), bf),
            pltpu.VMEM((2, hb + 1, tok, side), bf),
            pltpu.VMEM((2, 2, own, tok, side), bf),
            pltpu.VMEM((2, 2, own, tok, side), bf),
            pltpu.VMEM((nz - 1, hb, 2, kk, rows, side), bf),
        ]
        + [dma((2, own))] * 18
        + [dma((2, 2, kk)), dma((n1,)), dma((n1,))]
        + [dma((nz - 1, hb))] * 4
        + [dma((hb,))]
        + [dma((2,))] * 2,
        compiler_params=pltpu.CompilerParams(
            collective_id=0, has_side_effects=True, vmem_limit_bytes=67_000_000
        ),
    )(
        in_blocks, out_blocks, inverse(in_blocks), inverse(out_blocks),
        tokens, cotangent, w_in, w_out,
    )
    scale = 1.0 / math.sqrt(tok * ndp)
    wide = jnp.float32
    z = lax.axis_index("dp") // 2

    def both(part):
        return (part[0].astype(wide) + part[1].astype(wide)).astype(bf)

    def total(a):
        low = jnp.where(z > 0, red[1, a].astype(wide), 0.0)
        high = jnp.where(z < nz - 1, red[2, a].astype(wide), 0.0)
        return (red[0, a].astype(wide) + low + high) * scale

    return both(part_out), both(part_back), total(0), total(1)


def solution(mesh):
    ndp, nmp = mesh.shape["dp"], mesh.shape["mp"]

    def shards(tokens, cotangent, w_in, w_out, in_blocks, out_blocks):
        hb, kk, side, _ = w_in.shape
        blocks = tokens.shape[1] * nmp // side
        fits = (
            nmp == 4
            and ndp % 2 == 0
            and ndp > 4
            and kk == len(MASKS)
            and 2 * hb == blocks
            and hb % 8 == 0
            and side % (16 * ndp) == 0
        )
        args = (tokens, cotangent, w_in, w_out, in_blocks, out_blocks)
        if fits:
            return shards_fused(ndp, nmp, *args)
        return shards_plain(*args)

    placed = (
        P("dp", "mp"),
        P("dp", "mp"),
        P("mp", None, None, None),
        P("mp", None, None, None),
        P("mp", None),
        P("mp", None),
    )
    return jax.shard_map(
        shards,
        mesh=mesh,
        in_specs=placed,
        out_specs=(
            P("dp", "mp"),
            P("dp", "mp"),
            P("mp", None, "dp", None),
            P("mp", None, "dp", None),
        ),
        check_vma=False,
    )
```

```python
import functools
import math

import jax
import jax.numpy as jnp
from jax import lax
from jax.experimental import pallas as pl
from jax.experimental.pallas import tpu as pltpu
from jax.sharding import PartitionSpec as P

MB = 2
MASKS = (0, 1, 2, 4)
MESH = pl.DeviceIdType.MESH
C0 = math.sqrt(2.0 / math.pi)
C1 = 0.044715
SKEW = 2


def place_blocks(values, targets, row_blocks):
    step_tok = values.shape[0]
    side = values.shape[-1]
    flat = values.reshape(step_tok, -1, side)
    placed = (
        jnp.zeros((step_tok, row_blocks, side), jnp.float32).at[:, targets.reshape(-1)].add(flat)
    )
    return placed.reshape(step_tok, row_blocks * side)


def shards_plain(tokens, cotangent, w_in, w_out, in_blocks, out_blocks):
    hb_dev, kk, side, _ = w_in.shape
    total_tok = tokens.shape[0]
    width = tokens.shape[1] * lax.axis_size("mp")
    row_blocks = width // side
    passes = MB
    step_tok = total_tok // passes
    grad_in = jnp.zeros(w_in.shape, jnp.float32)
    grad_out = jnp.zeros(w_out.shape, jnp.float32)
    out_share = None
    outputs = []
    backs = []
    for index in range(passes):
        x_part = tokens[index * step_tok : (index + 1) * step_tok]
        dy_part = cotangent[index * step_tok : (index + 1) * step_tok]
        x_full = lax.all_gather(x_part, "mp", axis=1, tiled=True)
        selected = x_full.reshape(step_tok, row_blocks, side)[:, in_blocks]
        pre = jnp.einsum("tjkb,jkbc->tjc", selected, w_in, preferred_element_type=jnp.float32)
        act = jax.nn.gelu(pre).astype(jnp.bfloat16)
        terms = jnp.einsum("tjb,jkbc->tjkc", act, w_out, preferred_element_type=jnp.float32)
        partial_out = place_blocks(terms, out_blocks, row_blocks)
        outputs.append(
            lax.psum_scatter(
                partial_out.astype(jnp.bfloat16), "mp", scatter_dimension=1, tiled=True
            )
        )
        dy_full = lax.all_gather(dy_part, "mp", axis=1, tiled=True)
        picked = dy_full.reshape(step_tok, row_blocks, side)[:, out_blocks]
        d_act = jnp.einsum("tjkc,jkbc->tjb", picked, w_out, preferred_element_type=jnp.float32)
        _, pullback = jax.vjp(jax.nn.gelu, pre)
        d_pre = pullback(d_act)[0].astype(jnp.bfloat16)
        grad_out = grad_out + jnp.einsum(
            "tjb,tjkc->jkbc", act, picked, preferred_element_type=jnp.float32
        )
        grad_in = grad_in + jnp.einsum(
            "tjkb,tjc->jkbc", selected, d_pre, preferred_element_type=jnp.float32
        )
        back = jnp.einsum("tjc,jkbc->tjkb", d_pre, w_in, preferred_element_type=jnp.float32)
        partial_back = place_blocks(back, in_blocks, row_blocks)
        backs.append(
            lax.psum_scatter(
                partial_back.astype(jnp.bfloat16), "mp", scatter_dimension=1, tiled=True
            )
        )
    scale = 1.0 / math.sqrt(total_tok * lax.axis_size("dp"))
    in_share, out_share = (
        lax.psum_scatter(
            grad_in.astype(jnp.bfloat16), "dp", scatter_dimension=2, tiled=True
        ).astype(jnp.float32),
        lax.psum_scatter(
            grad_out.astype(jnp.bfloat16), "dp", scatter_dimension=2, tiled=True
        ).astype(jnp.float32),
    )
    output = jnp.concatenate(outputs, axis=0)
    grad_tokens = jnp.concatenate(backs, axis=0)
    return (output, grad_tokens, in_share * scale, out_share * scale)


def flip(u, m):
    if m == 0:
        return u
    return u + m * (1 - 2 * ((u // m) % 2))


def dot(a, b, dims):
    return lax.dot_general(a, b, (dims, ((), ())), preferred_element_type=jnp.float32)


def fused_kernel(
    dims,
    in_idx, out_idx, in_inv, out_inv, x_hbm, dy_hbm, win_hbm, wout_hbm,
    part_out, part_back, red,
    full, near, mine, theirs, arrived, act, dpre, act2, dpre2, wbuf, acc, csend, crecv, zbuf,
    own_sem, y_send, y_recv, c_send, c_recv, f_send, f_recv,
    x_send, x_recv, y2_send, y2_recv, c2_send, c2_recv, f2_send, f2_recv,
    p_send, p_recv, pl_sem,
    w_sem, g_send, g_recv, up_send, up_recv, dn_send, dn_recv, zl_sem,
    o_send, o_recv,
):
    ndp, nmp, hb, side, own, tok, rows, n1 = dims
    nz = ndp // 2
    dp = lax.axis_index("dp")
    mp = lax.axis_index("mp")
    z, mx = dp // 2, dp % 2
    y, core = mp // 2, mp % 2
    other_core = (dp, y * 2 + 1 - core)
    other_y = (dp, (1 - y) * 2 + core)
    other_x = (z * 2 + 1 - mx, mp)
    above = ((dp + 2) % ndp, mp)
    below = ((dp + ndp - 2) % ndp, mp)
    has_above = z < nz - 1
    has_below = z > 0
    g_core = other_core[1]
    g_y = other_y[1]
    g_far = (1 - y) * 2 + 1 - core
    srcs = (x_hbm, dy_hbm)
    parts = (part_out, part_back)
    nk = len(MASKS)

    barrier = pltpu.get_barrier_semaphore()
    peers = [other_core, other_y, other_x] + [((dp + 2 * dz) % ndp, mp) for dz in range(1, nz)]
    for peer in peers:
        pl.semaphore_signal(barrier, inc=1, device_id=peer, device_id_type=MESH)
    pl.semaphore_wait(barrier, len(peers))

    def remote(src, dst, ssem, rsem, peer):
        return pltpu.make_async_remote_copy(
            src_ref=src, dst_ref=dst, send_sem=ssem, recv_sem=rsem,
            device_id=peer, device_id_type=MESH,
        )

    def lanes(i):
        return pl.ds(pl.multiple_of(i * side, side), side)

    def piece(a, i):
        return srcs[a].at[:, lanes(i)]

    def to_y(a, i, slot):
        return remote(piece(a, i), full.at[a, slot * own + i], y_send.at[a, i], y_recv.at[a, i], other_y)

    def to_core(a, i, slot):
        return remote(piece(a, i), full.at[a, slot * own + i], c_send.at[a, i], c_recv.at[a, i], other_core)

    def forward(a, i, slot):
        return remote(
            full.at[a, g_y * own + i], full.at[a, slot * own + i],
            f_send.at[a, i], f_recv.at[a, i], other_core,
        )

    def to_near(a, i):
        return remote(piece(a, i), near.at[a, mp * own + i], x_send.at[a, i], x_recv.at[a, i], other_x)

    def near_y(a, i, slot):
        return remote(
            near.at[a, mp * own + i], near.at[a, slot * own + i],
            y2_send.at[a, i], y2_recv.at[a, i], other_y,
        )

    def near_core(a, i, slot):
        return remote(
            near.at[a, mp * own + i], near.at[a, slot * own + i],
            c2_send.at[a, i], c2_recv.at[a, i], other_core,
        )

    def near_forward(a, i, slot):
        return remote(
            near.at[a, g_y * own + i], near.at[a, slot * own + i],
            f2_send.at[a, i], f2_recv.at[a, i], other_core,
        )

    def keep(a, i):
        return pltpu.make_async_copy(piece(a, i), full.at[a, mp * own + i], own_sem.at[a, i])

    def w_copies(j, slot):
        return (
            pltpu.make_async_copy(win_hbm.at[j], wbuf.at[slot, 0], w_sem.at[slot, 0, 0]),
            pltpu.make_async_copy(wout_hbm.at[j], wbuf.at[slot, 1], w_sem.at[slot, 1, 0]),
        )

    def loop(n, body, first=0):
        lax.fori_loop(first, n, lambda i, c: (body(i), c)[1], 0)

    for a in range(2):
        def start(i, a=a):
            to_y(a, i, mp).start()
            to_near(a, i).start()
            to_core(a, i, mp).start()
            keep(a, i).start()
        loop(own, start)
    for cp in w_copies(0, 0):
        cp.start()
    for a in range(2):
        def relay(i, a=a):
            to_y(a, i, g_y).wait_recv()
            forward(a, i, g_y).start()
            to_near(a, i).wait_recv()
            near_y(a, i, mp).start()
            near_core(a, i, mp).start()
        loop(own, relay)
    for a in range(2):
        def settle(i, a=a):
            keep(a, i).wait()
            to_core(a, i, g_core).wait_recv()
            forward(a, i, g_far).wait_recv()
        loop(own, settle)

    def hidden_of(source, act_ref, dpre_ref):
        def hidden(j):
            slot = j % 2
            for cp in w_copies(j, slot):
                cp.wait()

            @pl.when(j + 1 < hb)
            def _():
                for cp in w_copies(j + 1, 1 - slot):
                    cp.start()

            pre = jnp.zeros((tok, side), jnp.float32)
            d_act = jnp.zeros((tok, side), jnp.float32)
            for k in range(nk):
                pre += dot(source[0, in_idx[j, k]], wbuf[slot, 0, k], ((1,), (0,)))
                d_act += dot(source[1, out_idx[j, k]], wbuf[slot, 1, k], ((1,), (1,)))
            th = jnp.tanh(C0 * (pre + C1 * (pre * pre * pre)))
            half = 0.5 * (1.0 + th)
            slope = half + 0.5 * pre * (1.0 - th * th) * (C0 * (1.0 + 3.0 * C1 * pre * pre))
            act_ref[j] = (pre * half).astype(jnp.bfloat16)
            dpre_ref[j] = (d_act * slope).astype(jnp.bfloat16)

        loop(hb, hidden)

    hidden_of(full, act, dpre)

    def to_x(j):
        return remote(theirs.at[j], arrived.at[j], g_send.at[j], g_recv.at[j], other_x)

    def split(value):
        value = value.astype(jnp.bfloat16).reshape(nz, 2, rows, side)
        low, high = value[:, 0], value[:, 1]
        return jnp.where(mx == 0, low, high), jnp.where(mx == 0, high, low)

    def weight_grads(j):
        for k in range(nk):
            gi = dot(full[0, in_idx[j, k]], dpre[j], ((0,), (0,)))
            go = dot(act[j], full[1, out_idx[j, k]], ((0,), (0,)))
            for a, value in ((0, gi), (1, go)):
                mine_half, their_half = split(value)
                mine[j, a, k] = mine_half
                theirs[j, a, k] = their_half
        to_x(j).start()

    loop(n1, weight_grads)

    def v_copies(u, slot):
        res = []
        for k, m in enumerate(MASKS):
            v = flip(u, m)
            res.append(pltpu.make_async_copy(win_hbm.at[v, k], wbuf.at[slot, 0, k], w_sem.at[slot, 0, k]))
            res.append(pltpu.make_async_copy(wout_hbm.at[v, k], wbuf.at[slot, 1, k], w_sem.at[slot, 1, k]))
        return res

    for cp in v_copies(0, 0):
        cp.start()

    def place(u):
        slot = u % 2
        for cp in v_copies(u, slot):
            cp.wait()

        @pl.when(u + 1 < hb)
        def _():
            for cp in v_copies(u + 1, 1 - slot):
                cp.start()

        out = jnp.zeros((tok, side), jnp.float32)
        back = jnp.zeros((tok, side), jnp.float32)
        for k, m in enumerate(MASKS):
            v = flip(u, m)
            out += dot(act[v], wbuf[slot, 1, k], ((1,), (0,)))
            back += dot(dpre[v], wbuf[slot, 0, k], ((1,), (1,)))
        acc[0, u] = out.astype(jnp.bfloat16)
        acc[1, u] = back.astype(jnp.bfloat16)

    loop(hb, place)
    for cp in w_copies(0, 0):
        cp.start()
    inv = (out_inv, in_inv)
    for a in range(2):
        acc[a, hb] = jnp.zeros((tok, side), jnp.bfloat16)

    def swap(a):
        return remote(csend.at[a], crecv.at[a], o_send.at[a], o_recv.at[a], other_core)

    for a in range(2):
        for yy in range(2):
            def fill(i, a=a, yy=yy):
                csend[a, yy, i] = acc[a, inv[a][(2 * yy + 1 - core) * own + i]]
            loop(own, fill)
        swap(a).start()

    def to_part(a, i):
        return remote(
            crecv.at[a, 1 - y, i], parts[a].at[1, :, lanes(i)], p_send.at[a, i], p_recv.at[a, i], other_y
        )

    def keep_part(a, i):
        return pltpu.make_async_copy(crecv.at[a, y, i], parts[a].at[0, :, lanes(i)], pl_sem.at[a, i])

    for a in range(2):
        swap(a).wait_recv()
        for yy in range(2):
            def join(i, a=a, yy=yy):
                crecv[a, yy, i] = crecv[a, yy, i] + acc[a, inv[a][(2 * yy + core) * own + i]]
            loop(own, join)

        def emit(i, a=a):
            to_part(a, i).start()
            keep_part(a, i).start()
        loop(own, emit)

    def up(j, u, last):
        dst = red.at[1, :, j] if last else zbuf.at[u - 1, j]
        return remote(mine.at[j, :, :, u], dst, up_send.at[u - 1, j], up_recv.at[u - 1, j], above)

    def down(j, u, last):
        dst = red.at[2, :, j] if last else zbuf.at[u, j]
        return remote(mine.at[j, :, :, u], dst, dn_send.at[u, j], dn_recv.at[u, j], below)

    def keep_z(j):
        return pltpu.make_async_copy(mine.at[j, :, :, z], red.at[0, :, j], zl_sem.at[j])

    def add_in(j, u, slot):
        for a in range(2):
            mine[j, a, :, u] = (
                mine[j, a, :, u].astype(jnp.float32) + zbuf[slot, j, a].astype(jnp.float32)
            ).astype(jnp.bfloat16)

    def hops(t):
        ju = t - SKEW * z
        jd = t - SKEW * (nz - 1 - z)
        up_ok = jnp.logical_and(ju >= 0, ju < hb)
        dn_ok = jnp.logical_and(jd >= 0, jd < hb)
        for u in range(nz - 1, 0, -1):
            @pl.when(jnp.logical_and(up_ok, z < u))
            def _(u=u):
                @pl.when(has_below)
                def _():
                    up(ju, u, False).wait_recv()
                    add_in(ju, u, u - 1)

                @pl.when(z == u - 1)
                def _():
                    up(ju, u, True).start()

                @pl.when(z < u - 1)
                def _():
                    up(ju, u, False).start()
        for u in range(nz - 1):
            @pl.when(jnp.logical_and(dn_ok, z > u))
            def _(u=u):
                @pl.when(has_above)
                def _():
                    down(jd, u, False).wait_recv()
                    add_in(jd, u, u)

                @pl.when(z == u + 1)
                def _():
                    down(jd, u, True).start()

                @pl.when(z > u + 1)
                def _():
                    down(jd, u, False).start()

    def first_steps(t):
        to_x(t).wait_recv()
        for a in range(2):
            for k in range(nk):
                mine[t, a, k] = (
                    mine[t, a, k].astype(jnp.float32) + arrived[t, a, k].astype(jnp.float32)
                ).astype(jnp.bfloat16)
        keep_z(t).start()
        hops(t)

    loop(n1, first_steps)

    for a in range(2):
        def relay2(i, a=a):
            near_y(a, i, g_y).wait_recv()
            near_forward(a, i, g_y).start()
        loop(own, relay2)
    for a in range(2):
        def settle2(i, a=a):
            near_core(a, i, g_core).wait_recv()
            near_forward(a, i, g_far).wait_recv()
        loop(own, settle2)

    hidden_of(near, act2, dpre2)

    def later_steps(t):
        for k in range(nk):
            gi = dot(full[0, in_idx[t, k]], dpre[t], ((0,), (0,)))
            gi += dot(near[0, in_idx[t, k]], dpre2[t], ((0,), (0,)))
            go = dot(act[t], full[1, out_idx[t, k]], ((0,), (0,)))
            go += dot(act2[t], near[1, out_idx[t, k]], ((0,), (0,)))
            mine[t, 0, k] = split(gi)[0]
            mine[t, 1, k] = split(go)[0]
        keep_z(t).start()
        hops(t)

    loop(hb, later_steps, n1)
    loop(hb + SKEW * (nz - 2), hops, hb)

    for a in range(2):
        def drain(i, a=a):
            to_y(a, i, mp).wait_send()
            to_core(a, i, mp).wait_send()
            forward(a, i, g_y).wait_send()
            to_near(a, i).wait_send()
            near_y(a, i, mp).wait_send()
            near_core(a, i, mp).wait_send()
            near_forward(a, i, g_y).wait_send()
            to_part(a, i).wait_send()
            to_part(a, i).wait_recv()
            keep_part(a, i).wait()
        loop(own, drain)
        swap(a).wait_send()

    def sent(j):
        to_x(j).wait_send()

    loop(n1, sent)

    def finish(j):
        keep_z(j).wait()
        for u in range(1, nz):
            @pl.when(z < u)
            def _(u=u):
                up(j, u, True).wait_send()

            @pl.when(z == u)
            def _(u=u):
                up(j, u, True).wait_recv()
        for u in range(nz - 1):
            @pl.when(z > u)
            def _(u=u):
                down(j, u, True).wait_send()

            @pl.when(z == u)
            def _(u=u):
                down(j, u, True).wait_recv()

    loop(hb, finish)


def shards_fused(ndp, nmp, tokens, cotangent, w_in, w_out, in_blocks, out_blocks):
    hb, kk, side, _ = w_in.shape
    tok, feats = tokens.shape
    own = feats // side
    blocks = own * nmp
    nz = ndp // 2
    rows = side // ndp
    n1 = 3 * hb // 16

    def inverse(table):
        hit = table[:, 0][None, :] == jnp.arange(blocks, dtype=jnp.int32)[:, None]
        where = jnp.sum(jnp.where(hit, jnp.arange(hb, dtype=jnp.int32)[None, :], 0), axis=1)
        return jnp.where(jnp.any(hit, axis=1), where, hb).astype(jnp.int32)

    bf = jnp.bfloat16
    any_spec = pl.BlockSpec(memory_space=pl.ANY)
    smem = pl.BlockSpec(memory_space=pltpu.SMEM)
    dma = pltpu.SemaphoreType.DMA
    part_out, part_back, red = pl.pallas_call(
        functools.partial(fused_kernel, (ndp, nmp, hb, side, own, tok, rows, n1)),
        out_shape=(
            jax.ShapeDtypeStruct((2, tok, feats), bf),
            jax.ShapeDtypeStruct((2, tok, feats), bf),
            jax.ShapeDtypeStruct((3, 2, hb, kk, rows, side), bf),
        ),
        in_specs=[smem] * 4 + [any_spec] * 4,
        out_specs=(any_spec,) * 3,
        scratch_shapes=[
            pltpu.VMEM((2, blocks, tok, side), bf),
            pltpu.VMEM((2, blocks, tok, side), bf),
            pltpu.VMEM((hb, 2, kk, nz, rows, side), bf),
            pltpu.VMEM((n1, 2, kk, nz, rows, side), bf),
            pltpu.VMEM((n1, 2, kk, nz, rows, side), bf),
            pltpu.VMEM((hb, tok, side), bf),
            pltpu.VMEM((hb, tok, side), bf),
            pltpu.VMEM((hb, tok, side), bf),
            pltpu.VMEM((hb, tok, side), bf),
            pltpu.VMEM((2, 2, kk, side, side), bf),
            pltpu.VMEM((2, hb + 1, tok, side), bf),
            pltpu.VMEM((2, 2, own, tok, side), bf),
            pltpu.VMEM((2, 2, own, tok, side), bf),
            pltpu.VMEM((nz - 1, hb, 2, kk, rows, side), bf),
        ]
        + [dma((2, own))] * 18
        + [dma((2, 2, kk)), dma((n1,)), dma((n1,))]
        + [dma((nz - 1, hb))] * 4
        + [dma((hb,))]
        + [dma((2,))] * 2,
        compiler_params=pltpu.CompilerParams(
            collective_id=0, has_side_effects=True, vmem_limit_bytes=67_000_000
        ),
    )(
        in_blocks, out_blocks, inverse(in_blocks), inverse(out_blocks),
        tokens, cotangent, w_in, w_out,
    )
    scale = 1.0 / math.sqrt(tok * ndp)
    wide = jnp.float32
    z = lax.axis_index("dp") // 2

    def both(part):
        return (part[0].astype(wide) + part[1].astype(wide)).astype(bf)

    def total(a):
        low = jnp.where(z > 0, red[1, a].astype(wide), 0.0)
        high = jnp.where(z < nz - 1, red[2, a].astype(wide), 0.0)
        return (red[0, a].astype(wide) + low + high) * scale

    return both(part_out), both(part_back), total(0), total(1)


def solution(mesh):
    ndp, nmp = mesh.shape["dp"], mesh.shape["mp"]

    def shards(tokens, cotangent, w_in, w_out, in_blocks, out_blocks):
        hb, kk, side, _ = w_in.shape
        blocks = tokens.shape[1] * nmp // side
        fits = (
            nmp == 4
            and ndp % 2 == 0
            and ndp > 4
            and kk == len(MASKS)
            and 2 * hb == blocks
            and hb % 8 == 0
            and side % (16 * ndp) == 0
        )
        args = (tokens, cotangent, w_in, w_out, in_blocks, out_blocks)
        if fits:
            return shards_fused(ndp, nmp, *args)
        return shards_plain(*args)

    placed = (
        P("dp", "mp"),
        P("dp", "mp"),
        P("mp", None, None, None),
        P("mp", None, None, None),
        P("mp", None),
        P("mp", None),
    )
    return jax.shard_map(
        shards,
        mesh=mesh,
        in_specs=placed,
        out_specs=(
            P("dp", "mp"),
            P("dp", "mp"),
            P("mp", None, "dp", None),
            P("mp", None, "dp", None),
        ),
        check_vma=False,
    )
```
